32 devices in a mesh: parts: 2 (over y), row: 4 (over x, core), col: 4 (over z).
Axes of the slice: x: 2, y: 2, z: 4, core: 2. Of those that a mesh axis runs over, the one named last changes fastest.
Arguments:
- latent: bfloat16 [4, 32, 32, 640], P('parts', 'row', 'col'), parts along dimension 0, may hold values from -6 to 6
- timestep: int32 [4], P('parts'), parts along dimension 0, may hold values from 0 to 999
- gn_gain: float32 [640], replicated, may hold values from 0.25 to 1.75
- gn_bias: float32 [640], replicated, may hold values from -3 to 3
- conv_weight: bfloat16 [3, 3, 640, 640], P(None, None, None, 'row'), may hold values from -0.078125 to 0.078125
- conv_bias: float32 [640], replicated, may hold values from -3 to 3
- time_weight: bfloat16 [320, 640], replicated, may hold values from -0.625 to 0.625
- ln_gain: float32 [640], replicated, may hold values from 0.25 to 1.75
- q_weight: bfloat16 [640, 384], replicated, may hold values from -0.5 to 0.5
- k_weight: bfloat16 [640, 384], replicated, may hold values from -0.25 to 0.25
- v_weight: bfloat16 [640, 384], replicated, may hold values from -0.25 to 0.25
- out_weight: bfloat16 [384, 640], replicated, may hold values from -0.3125 to 0.3125
- stale_keys: bfloat16 [4, 32, 32, 384], P('parts', 'row', 'col'), parts along dimension 0, may hold values from -40 to 40
- stale_values: bfloat16 [4, 32, 32, 384], P('parts', 'row', 'col'), parts along dimension 0, may hold values from -6 to 6
Outputs:
- mixed: bfloat16 [4, 32, 32, 640], P('parts', 'row', 'col'), parts along dimension 0
- fresh_keys: bfloat16 [4, 32, 32, 384], P('parts', 'row', 'col'), parts along dimension 0
- fresh_values: bfloat16 [4, 32, 32, 384], P('parts', 'row', 'col'), parts along dimension 0
The draws below stay inside these ranges and needn't reach their ends.
There are 2 independent parts, one for each index of `parts`. The reference program is written for one: setup_inputs(seed, part) draws one part's arguments, and reference() takes and returns one part's arrays. A program takes and returns all parts, laid end to end along the dimension named above; an argument that names none is the same for every part. Nothing has to cross between parts.
All inputs are finite; a program needn't handle non-finite values.
Results may differ from the reference program's by a relative error of at most 0.012.
Values may be sent and summed in bfloat16 or wider, within the bound.
A program may use at most 64 MiB of HBM per device.

```python
import jax
import jax.numpy as jnp
from jax import lax

C = 640
NH = 6
HD = 64
GROUPS = 32
TDIM = 320
IMAGE_GROUP_SIZE = 2
RD = 8
CD = 8
GRID_HEIGHT = 32
GRID_WIDTH = 32
INNER = 384
N_ROW = 4
N_COL = 4


def draw_stale_keys(key, part):
    first = jax.random.fold_in(key, 0)
    shape = (IMAGE_GROUP_SIZE, GRID_HEIGHT, GRID_WIDTH, NH * HD)
    result = jnp.clip(jax.random.normal(first, shape, jnp.float32), -6.0, 6.0)
    return result.astype(jnp.bfloat16)


def draw_q_weight(key, part):
    first = jax.random.fold_in(key, 0)
    scale = 1.0 / jnp.sqrt(jnp.float32(C))
    starting_level = jnp.clip(jax.random.normal(first, (C, NH * HD), jnp.float32), -6.0, 6.0) * scale
    return jnp.clip(starting_level, -0.5, 0.5).astype(jnp.bfloat16)


def block_levels(stream_key, shape, pieces, least, high):
    level = 1.0
    for dim, parts in pieces:
        heights = jax.random.uniform(jax.random.fold_in(jax.random.fold_in(stream_key, 6), dim), (parts,), jnp.float32, least / len(pieces), high / len(pieces))
        level = level * jnp.repeat(jnp.exp(heights), shape[dim] // parts).reshape((-1,) + (1,) * (len(shape) - 1 - dim))
    return level


def scatter_about(stream_key, extent, scale, limit, cuts=(), held_as=jnp.bfloat16):
    values = scale * jax.random.normal(stream_key, extent, jnp.float32)
    if cuts:
        values = values * block_levels(stream_key, extent, cuts, -0.22, 0.18)
    return jnp.clip(values, -limit, limit).astype(held_as)


def setup_inputs(seed: int = 0, part: int = 0) -> dict:
    keys = jax.random.split(jax.random.key(seed), 15)
    part_splits = jax.random.split(jax.random.fold_in(keys[14], part), 15)
    latent = scatter_about(part_splits[0], (IMAGE_GROUP_SIZE, GRID_HEIGHT, GRID_WIDTH, C), 1.0, 6.0, ((1, 4), (2, 4)))
    timestep = jax.random.randint(part_splits[1], (IMAGE_GROUP_SIZE,), 0, 1000).astype(jnp.int32)
    gn_gain = jnp.clip(1.0 + 0.15 * jax.random.normal(keys[2], (C,), jnp.float32), 0.25, 1.75)
    gn_bias = scatter_about(keys[3], (C,), 0.5, 3.0, (), jnp.float32)
    conv_weight = scatter_about(keys[4], (3, 3, C, C), (9 * C) ** -0.5, 0.078125, ((3, 4),))
    conv_bias = scatter_about(keys[5], (C,), 0.5, 3.0, (), jnp.float32)
    time_weight = scatter_about(keys[6], (TDIM, C), (TDIM // 4) ** -0.5, 0.625)
    ln_gain = jnp.clip(1.0 + 0.15 * jax.random.normal(keys[7], (C,), jnp.float32), 0.25, 1.75)
    q_weight = draw_q_weight(jax.random.fold_in(keys[14], 71), part)
    k_weight = scatter_about(keys[9], (C, INNER), C ** -0.5, 0.25)
    v_weight = scatter_about(keys[10], (C, INNER), C ** -0.5, 0.25)
    out_weight = scatter_about(keys[11], (INNER, C), INNER ** -0.5, 0.3125)
    stale_keys = draw_stale_keys(jax.random.fold_in(jax.random.fold_in(keys[14], part), 71), part)
    stale_values = scatter_about(part_splits[13], (IMAGE_GROUP_SIZE, GRID_HEIGHT, GRID_WIDTH, INNER), 1.0, 6.0, ((1, 4), (2, 4)))
    return dict(latent=latent, timestep=timestep, gn_gain=gn_gain, gn_bias=gn_bias, conv_weight=conv_weight, conv_bias=conv_bias, time_weight=time_weight, ln_gain=ln_gain, q_weight=q_weight, k_weight=k_weight, v_weight=v_weight, out_weight=out_weight, stale_keys=stale_keys, stale_values=stale_values)


def time_features(timestep):
    half = TDIM // 2
    freqs = jnp.exp(-jnp.log(10000.0) * jnp.arange(half, dtype=jnp.float32) / half)
    angles = timestep.astype(jnp.float32)[:, None] * freqs[None, :]
    return jnp.concatenate([jnp.cos(angles), jnp.sin(angles)], axis=1)

def to_patches(array):
    batch = array.shape[0]
    shaped = array.reshape(batch, N_ROW, RD, N_COL, CD, NH, HD)
    return shaped.transpose(0, 1, 3, 2, 4, 5, 6).reshape(batch, N_ROW * N_COL, RD * CD, NH, HD)

def from_patches(array):
    batch = array.shape[0]
    shaped = array.reshape(batch, N_ROW, N_COL, RD, CD, NH * HD)
    return shaped.transpose(0, 1, 3, 2, 4, 5).reshape(batch, GRID_HEIGHT, GRID_WIDTH, NH * HD)

def one_image(items):
    query_p, fresh_kp, fresh_vp, stale_k, stale_v = items
    patches = query_p.shape[0]
    span = query_p.shape[1]
    keys_flat = stale_k.reshape(patches * span, NH, HD).astype(jnp.float32)
    values_flat = stale_v.reshape(patches * span, NH, HD).astype(jnp.float32)
    owner = jnp.arange(patches * span, dtype=jnp.int32) // span

    def one_patch(index):
        query = query_p[index].astype(jnp.float32)
        fresh_k = fresh_kp[index].astype(jnp.float32)
        fresh_v = fresh_vp[index].astype(jnp.float32)
        masked = (owner == index)[None, None, :]
        scores = jnp.einsum('qhd,khd->hqk', query, keys_flat)
        scores = jnp.where(masked, -1e+30, scores)
        own_scores = jnp.einsum('qhd,khd->hqk', query, fresh_k)
        peak = jnp.maximum(lax.optimization_barrier(jnp.max(scores, axis=-1)), lax.optimization_barrier(jnp.max(own_scores, axis=-1)))
        weights = jnp.where(masked, 0.0, jnp.exp(scores - peak[..., None]))
        own_weights = jnp.exp(own_scores - peak[..., None])
        total = lax.optimization_barrier(jnp.sum(weights, axis=-1)) + lax.optimization_barrier(jnp.sum(own_weights, axis=-1))
        rounded = weights.astype(jnp.bfloat16).astype(jnp.float32)
        own_rounded = own_weights.astype(jnp.bfloat16).astype(jnp.float32)
        summed = jnp.einsum('hqk,khd->hqd', rounded, values_flat) + jnp.einsum('hqk,khd->hqd', own_rounded, fresh_v)
        result = summed / total[..., None]
        return result.transpose(1, 0, 2).reshape(span, NH * HD).astype(jnp.bfloat16)
    return lax.map(one_patch, jnp.arange(patches, dtype=jnp.int32))

def reference(latent, timestep, gn_gain, gn_bias, conv_weight, conv_bias, time_weight, ln_gain, q_weight, k_weight, v_weight, out_weight, stale_keys, stale_values):
    batch = latent.shape[0]
    emb = jax.nn.silu(time_features(timestep)).astype(jnp.bfloat16)
    temb = jnp.dot(emb, time_weight, preferred_element_type=jnp.float32)
    values = latent.astype(jnp.float32)
    grouped = values.reshape(batch, GRID_HEIGHT * GRID_WIDTH, GROUPS, C // GROUPS)
    mean = lax.optimization_barrier(jnp.mean(grouped, axis=(1, 3)))
    var = lax.optimization_barrier(jnp.mean(grouped * grouped, axis=(1, 3))) - mean * mean
    normed = (grouped - mean[:, None, :, None]) * lax.rsqrt(var + 1e-05)[:, None, :, None]
    normed = normed.reshape(batch, GRID_HEIGHT, GRID_WIDTH, C) * gn_gain + gn_bias
    act = jax.nn.silu(normed).astype(jnp.bfloat16)
    padded = jnp.pad(act, ((0, 0), (1, 1), (1, 1), (0, 0)))
    conv = jnp.zeros((batch, GRID_HEIGHT, GRID_WIDTH, C), jnp.float32)
    for down in range(3):
        for across in range(3):
            conv = conv + jnp.dot(padded[:, down:down + GRID_HEIGHT, across:across + GRID_WIDTH, :], conv_weight[down, across], preferred_element_type=jnp.float32)
    hidden = (values + conv + conv_bias + temb[:, None, None, :]).astype(jnp.bfloat16)
    hidden_f = hidden.astype(jnp.float32)
    centre = hidden_f - lax.optimization_barrier(jnp.mean(hidden_f, axis=-1, keepdims=True))
    spread = lax.optimization_barrier(jnp.mean(centre * centre, axis=-1, keepdims=True))
    layer_normed = (centre * lax.rsqrt(spread + 1e-05) * ln_gain).astype(jnp.bfloat16)
    queries = (jnp.dot(layer_normed, q_weight, preferred_element_type=jnp.float32) * (1.0 / jnp.sqrt(jnp.float32(HD)))).astype(jnp.bfloat16)
    fresh_keys = jnp.dot(layer_normed, k_weight, preferred_element_type=jnp.float32).astype(jnp.bfloat16)
    fresh_values = jnp.dot(layer_normed, v_weight, preferred_element_type=jnp.float32).astype(jnp.bfloat16)
    attended = lax.map(one_image, (to_patches(queries), to_patches(fresh_keys), to_patches(fresh_values), to_patches(stale_keys), to_patches(stale_values)))
    attn = from_patches(attended)
    mixed = (hidden_f + jnp.dot(attn, out_weight, preferred_element_type=jnp.float32)).astype(jnp.bfloat16)
    return (mixed, fresh_keys, fresh_values)
```

```python
import functools

import jax
import jax.numpy as jnp
from jax import lax
from jax.experimental import pallas as pl
from jax.experimental.pallas import tpu as pltpu
from jax.sharding import PartitionSpec as P

HD = 64
GROUPS = 32
PAIR = 2
MESH = pl.DeviceIdType.MESH
F32 = jnp.float32
BF16 = jnp.bfloat16


def time_features(timestep, width):
    half = width // 2
    freqs = jnp.exp(-jnp.log(10000.0) * jnp.arange(half, dtype=jnp.float32) / half)
    angles = timestep.astype(jnp.float32)[:, None] * freqs[None, :]
    return jnp.concatenate([jnp.cos(angles), jnp.sin(angles)], axis=1)


def group_total(sums, size):
    width = sums.shape[1]
    lane = lax.broadcasted_iota(jnp.int32, sums.shape, 1)

    def window(x, sign):
        parts, total, offset = {1: x}, None, 0
        step = 1
        while step * 2 <= size:
            last = parts[step]
            parts[step * 2] = last + pltpu.roll(last, (sign * step) % width, 1)
            step *= 2
        for step in sorted(parts, reverse=True):
            if size & step:
                piece = parts[step]
                if offset:
                    piece = pltpu.roll(piece, (sign * offset) % width, 1)
                total = piece if total is None else total + piece
                offset += step
        return total

    ends = jnp.where(lax.rem(lane, size) == size - 1, window(sums, 1), 0.0)
    return window(ends, -1)


def kernel(
    dims,
    lat_ref,
    edge_ref,
    tb_ref,
    gg_ref,
    gb_ref,
    lg_ref,
    cw_hbm,
    qw_hbm,
    kw_hbm,
    vw_hbm,
    ow_hbm,
    sk_hbm,
    sv_hbm,
    mixed_ref,
    fk_ref,
    fv_ref,
    band,
    halo,
    acts,
    raw,
    cw,
    qkvw,
    ow,
    stats,
    hsend,
    hbuf,
    hfull,
    kbuf,
    vbuf,
    qown,
    qin,
    own_o,
    own_s,
    out_o,
    out_s,
    in_o,
    in_s,
    attn,
    load_sem,
    row_send,
    row_recv,
    col_send,
    col_recv,
    edge_send,
    edge_recv,
    fwd_send,
    fwd_recv,
    x_send,
    x_recv,
):
    R, C, NX, rows, cols, channels, inner, count_all = dims
    span = rows * cols
    wide = channels // R
    nb = 2
    me = lax.axis_index("row")
    mc = lax.axis_index("col")

    def remote(src, dst, send, recv, **where):
        return pltpu.make_async_remote_copy(
            src_ref=src, dst_ref=dst, send_sem=send, recv_sem=recv, device_id=where, device_id_type=MESH
        )

    loads = [
        pltpu.make_async_copy(cw_hbm, cw, load_sem.at[0]),
        pltpu.make_async_copy(qw_hbm, qkvw.at[:, 0:inner], load_sem.at[1]),
        pltpu.make_async_copy(kw_hbm, qkvw.at[:, inner : 2 * inner], load_sem.at[2]),
        pltpu.make_async_copy(vw_hbm, qkvw.at[:, 2 * inner : 3 * inner], load_sem.at[3]),
        pltpu.make_async_copy(ow_hbm, ow, load_sem.at[4]),
        pltpu.make_async_copy(sk_hbm, kbuf.at[:, 0:span], load_sem.at[5]),
        pltpu.make_async_copy(sv_hbm, vbuf.at[:, 0:span], load_sem.at[6]),
    ]
    for load in loads:
        load.start()

    barrier = pltpu.get_barrier_semaphore()
    for d in range(1, R):
        pl.semaphore_signal(barrier, inc=1, device_id={"row": lax.rem(me + d, R)}, device_id_type=MESH)
    for d in range(1, C):
        pl.semaphore_signal(barrier, inc=1, device_id={"col": lax.rem(mc + d, C)}, device_id_type=MESH)
    pl.semaphore_wait(barrier, R - 1 + C - 1)

    to_right = remote(edge_ref.at[0], halo.at[me, 0], edge_send.at[0], edge_recv.at[0], col=lax.rem(mc + 1, C))
    to_left = remote(edge_ref.at[1], halo.at[me, 1], edge_send.at[1], edge_recv.at[1], col=lax.rem(mc + C - 1, C))

    @pl.when(mc < C - 1)
    def _():
        to_right.start()

    @pl.when(mc > 0)
    def _():
        to_left.start()

    lat_out = []
    for d in range(1, R):
        copy = remote(lat_ref, band.at[me], row_send.at[0, d], row_recv.at[0, d], row=lax.rem(me + d, R))
        copy.start()
        lat_out.append(copy)
    band[me] = lat_ref[...]

    @pl.when(mc == 0)
    def _():
        halo[me, 0] = jnp.zeros(halo.shape[2:], F32)

    @pl.when(mc == C - 1)
    def _():
        halo[me, 1] = jnp.zeros(halo.shape[2:], F32)

    @pl.when(mc > 0)
    def _():
        to_right.wait_recv()

    @pl.when(mc < C - 1)
    def _():
        to_left.wait_recv()

    halo_out = []
    for d in range(1, R):
        copy = remote(halo.at[me], halo.at[me], row_send.at[1, d], row_recv.at[1, d], row=lax.rem(me + d, R))
        copy.start()
        halo_out.append(copy)
    for copy in lat_out:
        copy.wait_recv()

    one = [jnp.zeros((cols, channels), F32) for _ in range(nb)]
    two = [jnp.zeros((cols, channels), F32) for _ in range(nb)]
    for r in range(R):
        halves = []
        for b in range(nb):
            x = band[r, b].astype(F32)
            one[b] = one[b] + jnp.sum(x, axis=0)
            two[b] = two[b] + jnp.sum(x * x, axis=0)
            halves.append(x)
        raw[r * rows : (r + 1) * rows] = jnp.concatenate(halves, axis=1).astype(BF16)
    rows_of = [jnp.sum(x, axis=0, keepdims=True) for x in one + two]
    stats[0] = jnp.concatenate(rows_of + rows_of, axis=0)
    stat_out = []
    for d in range(1, C):
        copy = remote(
            stats.at[0], stats.at[C - d], col_send.at[0, d], col_recv.at[0, d], col=lax.rem(mc + d, C)
        )
        copy.start()
        stat_out.append(copy)
    loads[5].wait()
    loads[6].wait()
    stale_out = []
    for d in range(1, C):
        for n, buf in ((1, kbuf), (2, vbuf)):
            copy = remote(
                buf.at[:, 0:span],
                buf.at[:, (C - d) * span : (C - d + 1) * span],
                col_send.at[n, d],
                col_recv.at[n, d],
                col=lax.rem(mc + d, C),
            )
            copy.start()
            stale_out.append(copy)
    pick = (
        lax.broadcasted_iota(jnp.int32, (channels, wide), 0)
        == lax.broadcasted_iota(jnp.int32, (channels, wide), 1) + me * wide
    )
    acc = jnp.dot(
        raw[...].reshape(R * rows * nb * cols, channels),
        jnp.where(pick, 1.0, 0.0).astype(BF16),
        preferred_element_type=F32,
    )
    for copy in stat_out:
        copy.wait_recv()
    total = stats[0]
    for d in range(1, C):
        total = total + stats[d]
    total = group_total(total, channels // GROUPS) * (1.0 / count_all)
    mean = [total[b : b + 1] for b in range(nb)]
    scale = [lax.rsqrt(total[nb + b : nb + b + 1] - mean[b] * mean[b] + 1e-05) * gg_ref[...] for b in range(nb)]
    bias = gb_ref[...]

    def activate(x, b):
        y = (x - mean[b]) * scale[b] + bias
        return y * jax.nn.sigmoid(y)

    for copy in halo_out:
        copy.wait_recv()
    place = lax.broadcasted_iota(jnp.int32, (rows, cols, channels), 1)
    for t in range(3):
        acts[t, 0] = jnp.zeros(acts.shape[2:], BF16)
        acts[t, R * rows + 1] = jnp.zeros(acts.shape[2:], BF16)
    for r in range(R):
        tap = [[], [], []]
        for b in range(nb):
            a = activate(band[r, b].astype(F32), b)
            left = jnp.where(mc > 0, activate(halo[r, 0, b], b), 0.0)
            right = jnp.where(mc < C - 1, activate(halo[r, 1, b], b), 0.0)
            tap[0].append(jnp.where(place == 0, left, pltpu.roll(a, 1, 1)))
            tap[1].append(a)
            tap[2].append(jnp.where(place == cols - 1, right, pltpu.roll(a, cols - 1, 1)))
        for t in range(3):
            acts[t, 1 + r * rows : 1 + (r + 1) * rows] = jnp.concatenate(tap[t], axis=1).astype(BF16)
    loads[0].wait()
    for across in range(3):
        for down in range(3):
            acc = acc + jnp.dot(
                acts[across, down : down + R * rows].reshape(R * rows * nb * cols, channels),
                cw[down, across],
                preferred_element_type=F32,
            )
    hid = acc.reshape(R * rows, nb * cols, wide) + tb_ref[...][None]
    hsend[...] = hid.reshape(R, nb * span, wide).astype(BF16)
    h_out = []
    for d in range(1, R):
        to = lax.rem(me + d, R)
        copy = remote(hsend.at[to], hbuf.at[me], row_send.at[2, d], row_recv.at[2, d], row=to)
        copy.start()
        h_out.append(copy)
    hbuf[me] = hsend[me]
    for copy in stale_out:
        copy.wait_recv()
    mate = me + 1 - 2 * lax.rem(me, PAIR)
    forwards = []
    for n, buf in enumerate((kbuf, vbuf)):
        copy = remote(
            buf.at[:, 0 : C * span], buf.at[:, C * span : 2 * C * span], fwd_send.at[n], fwd_recv.at[n], row=mate
        )
        copy.start()
        forwards.append(copy)
    for copy in h_out:
        copy.wait_recv()
    h = jnp.concatenate([hbuf[r].astype(F32) for r in range(R)], axis=1)
    hfull[...] = h
    centre = h - jnp.mean(h, axis=1, keepdims=True)
    spread = jnp.mean(centre * centre, axis=1, keepdims=True)
    normed = (centre * lax.rsqrt(spread + 1e-05) * lg_ref[...]).astype(BF16)
    for n in (1, 2, 3):
        loads[n].wait()
    qkv = jnp.dot(normed, qkvw[...], preferred_element_type=F32).reshape(rows, nb, cols, 3 * inner)
    for b in range(nb):
        part = qkv[:, b].reshape(span, 3 * inner)
        qown[b] = (part[:, 0:inner] * (1.0 / HD**0.5)).astype(BF16)
        k = part[:, inner : 2 * inner].astype(BF16)
        v = part[:, 2 * inner :].astype(BF16)
        kbuf[b, 2 * C * span :] = k
        vbuf[b, 2 * C * span :] = v
        fk_ref[b] = k
        fv_ref[b] = v
    q_out = []
    for d in range(1, NX):
        copy = remote(
            qown, qin.at[NX - d], x_send.at[0, d], x_recv.at[0, d], row=lax.rem(me + d * PAIR, R)
        )
        copy.start()
        q_out.append(copy)
    for copy in forwards:
        copy.wait_recv()

    half = lax.broadcasted_iota(jnp.int32, (span, 2 * HD), 1) < HD
    lanes = lax.broadcasted_iota(jnp.int32, (span, 128), 1)
    zero = jnp.zeros((span, 2 * HD), BF16)

    def attend(q, b, start, o_store):
        held = jnp.zeros((span, 128), F32)
        for pair in range(inner // (2 * HD)):
            at = slice(pair * 2 * HD, (pair + 1) * 2 * HD)
            q2 = q[:, at]
            q2 = jnp.concatenate([jnp.where(half, q2, zero), jnp.where(half, zero, q2)], axis=0)
            s = lax.dot_general(
                q2, kbuf[b, start : start + 2 * C * span, at], (((1,), (1,)), ((), ())), preferred_element_type=F32
            )
            m = jnp.max(s, axis=1, keepdims=True)
            p = jnp.exp(s - m)
            l = jnp.sum(p, axis=1, keepdims=True)
            o = jnp.dot(p.astype(BF16), vbuf[b, start : start + 2 * C * span, at], preferred_element_type=F32)
            o_store(at, jnp.where(half, o[:span], o[span:]))
            for n in range(2):
                held = jnp.where(lanes == pair * 2 + n, m[n * span : (n + 1) * span], held)
                held = jnp.where(lanes == 64 + pair * 2 + n, l[n * span : (n + 1) * span], held)
        return held

    for b in range(nb):

        def keep(at, o, b=b):
            own_o[b, :, at] = o

        own_s[b] = attend(qown[b], b, span, keep)

    back = []
    for d in range(1, NX):
        q_out[NX - 1 - d].wait_recv()
        for b in range(nb):

            def give(at, o, b=b, d=d):
                out_o[d, b, :, at] = o.astype(BF16)

            out_s[d, b] = attend(qin[d, b], b, 0, give)
        to = lax.rem(me + d * PAIR, R)
        for n, src, dst in ((1, out_o, in_o), (2, out_s, in_s)):
            copy = remote(src.at[d], dst.at[NX - d], x_send.at[n, d], x_recv.at[n, d], row=to)
            copy.start()
            back.append(copy)
    for copy in back:
        copy.wait_recv()
    loads[4].wait()
    for b in range(nb):
        for pair in range(inner // (2 * HD)):
            at = slice(pair * 2 * HD, (pair + 1) * 2 * HD)

            def spread_of(held, base):
                one_of = held[:, base + pair * 2 : base + pair * 2 + 1]
                two_of = held[:, base + pair * 2 + 1 : base + pair * 2 + 2]
                return jnp.where(half, one_of, two_of)

            helds = [own_s[b]] + [in_s[d, b] for d in range(1, NX)]
            sums = [own_o[b, :, at]] + [in_o[d, b, :, at].astype(F32) for d in range(1, NX)]
            peaks = [spread_of(held, 0) for held in helds]
            top = functools.reduce(jnp.maximum, peaks)
            num, den = 0.0, 0.0
            for held, o, peak in zip(helds, sums, peaks):
                factor = jnp.exp(peak - top)
                num = num + o * factor
                den = den + spread_of(held, 64) * factor
            attn[b, :, at] = (num / den).astype(BF16)
        hb = hfull[...].reshape(rows, nb, cols, channels)[:, b].reshape(span, channels)
        mixed_ref[b] = (hb + jnp.dot(attn[b], ow[...], preferred_element_type=F32)).astype(BF16)

    @pl.when(mc < C - 1)
    def _():
        to_right.wait_send()

    @pl.when(mc > 0)
    def _():
        to_left.wait_send()

    for copy in lat_out + halo_out + stat_out + stale_out + h_out + forwards + q_out + back:
        copy.wait_send()


def body(
    latent,
    timestep,
    gn_gain,
    gn_bias,
    conv_weight,
    conv_bias,
    time_weight,
    ln_gain,
    q_weight,
    k_weight,
    v_weight,
    out_weight,
    stale_keys,
    stale_values,
):
    batch, rows, cols, channels = latent.shape
    inner = q_weight.shape[1]
    R, C = lax.axis_size("row"), lax.axis_size("col")
    NX = R // PAIR
    span = rows * cols
    wide = conv_weight.shape[3]
    count_all = span * R * C * (channels // GROUPS)
    me = lax.axis_index("row")
    emb = jax.nn.silu(time_features(timestep, time_weight.shape[0])).astype(BF16)
    temb = jnp.dot(emb, time_weight, preferred_element_type=F32) + conv_bias
    temb = lax.dynamic_slice_in_dim(temb, me * wide, wide, 1)
    temb = jnp.repeat(temb, cols, axis=0)
    edges = jnp.stack([latent[:, :, cols - 1], latent[:, :, 0]]).astype(F32)[:, :, :, None, :]
    vm = pl.BlockSpec(memory_space=pltpu.VMEM)
    hbm = pl.BlockSpec(memory_space=pl.ANY)
    dma = pltpu.SemaphoreType.DMA
    mixed, fresh_k, fresh_v = pl.pallas_call(
        functools.partial(kernel, (R, C, NX, rows, cols, channels, inner, count_all)),
        out_shape=(
            jax.ShapeDtypeStruct((batch, span, channels), BF16),
            jax.ShapeDtypeStruct((batch, span, inner), BF16),
            jax.ShapeDtypeStruct((batch, span, inner), BF16),
        ),
        in_specs=[vm] * 6 + [hbm] * 7,
        out_specs=(vm, vm, vm),
        scratch_shapes=[
            pltpu.VMEM((R, batch, rows, cols, channels), BF16),
            pltpu.VMEM((R, 2, batch, rows, 1, channels), F32),
            pltpu.VMEM((3, R * rows + 2, batch * cols, channels), BF16),
            pltpu.VMEM((R * rows, batch * cols, channels), BF16),
            pltpu.VMEM(conv_weight.shape, BF16),
            pltpu.VMEM((channels, 3 * inner), BF16),
            pltpu.VMEM((inner, channels), BF16),
            pltpu.VMEM((C, 8, channels), F32),
            pltpu.VMEM((R, batch * span, wide), BF16),
            pltpu.VMEM((R, batch * span, wide), BF16),
            pltpu.VMEM((batch * span, channels), F32),
            pltpu.VMEM((batch, (2 * C + 1) * span, inner), BF16),
            pltpu.VMEM((batch, (2 * C + 1) * span, inner), BF16),
            pltpu.VMEM((batch, span, inner), BF16),
            pltpu.VMEM((NX, batch, span, inner), BF16),
            pltpu.VMEM((batch, span, inner), F32),
            pltpu.VMEM((batch, span, 128), F32),
            pltpu.VMEM((NX, batch, span, inner), BF16),
            pltpu.VMEM((NX, batch, span, 128), F32),
            pltpu.VMEM((NX, batch, span, inner), BF16),
            pltpu.VMEM((NX, batch, span, 128), F32),
            pltpu.VMEM((batch, span, inner), BF16),
            dma((7,)),
            dma((3, R)),
            dma((3, R)),
            dma((3, C)),
            dma((3, C)),
            dma((2,)),
            dma((2,)),
            dma((2,)),
            dma((2,)),
            dma((3, NX)),
            dma((3, NX)),
        ],
        compiler_params=pltpu.CompilerParams(
            collective_id=0, has_side_effects=True, vmem_limit_bytes=56 * 1024 * 1024
        ),
    )(
        latent,
        edges,
        temb,
        gn_gain.reshape(1, channels),
        gn_bias.reshape(1, channels),
        ln_gain.reshape(1, channels),
        conv_weight,
        q_weight,
        k_weight,
        v_weight,
        out_weight,
        stale_keys.reshape(batch, span, inner),
        stale_values.reshape(batch, span, inner),
    )
    return (
        mixed.reshape(batch, rows, cols, channels),
        fresh_k.reshape(batch, rows, cols, inner),
        fresh_v.reshape(batch, rows, cols, inner),
    )


def solution(mesh):
    placed = (
        P("parts", "row", "col", None),
        P("parts"),
        P(),
        P(),
        P(None, None, None, "row"),
        P(),
        P(),
        P(),
        P(),
        P(),
        P(),
        P(),
        P("parts", "row", "col", None),
        P("parts", "row", "col", None),
    )
    return jax.shard_map(
        body,
        mesh=mesh,
        in_specs=placed,
        out_specs=(
            P("parts", "row", "col", None),
            P("parts", "row", "col", None),
            P("parts", "row", "col", None),
        ),
        check_vma=False,
    )
```

```python
import functools

import jax
import jax.numpy as jnp
from jax import lax
from jax.experimental import pallas as pl
from jax.experimental.pallas import tpu as pltpu
from jax.sharding import PartitionSpec as P

HD = 64
GROUPS = 32
PAIR = 2
EARLY = True
MESH = pl.DeviceIdType.MESH
F32 = jnp.float32
BF16 = jnp.bfloat16


def group_total(sums, size):
    width = sums.shape[1]
    lane = lax.broadcasted_iota(jnp.int32, sums.shape, 1)

    def window(x, sign):
        parts, total, offset = {1: x}, None, 0
        step = 1
        while step * 2 <= size:
            last = parts[step]
            parts[step * 2] = last + pltpu.roll(last, (sign * step) % width, 1)
            step *= 2
        for step in sorted(parts, reverse=True):
            if size & step:
                piece = parts[step]
                if offset:
                    piece = pltpu.roll(piece, (sign * offset) % width, 1)
                total = piece if total is None else total + piece
                offset += step
        return total

    ends = jnp.where(lax.rem(lane, size) == size - 1, window(sums, 1), 0.0)
    return window(ends, -1)


def send_stale(go, kbuf, vbuf, span, C, mc, col_send, col_recv):
    return [
        go(
            buf.at[:, 0:span],
            buf.at[:, (C - d) * span : (C - d + 1) * span],
            col_send.at[n, d],
            col_recv.at[n, d],
            col=lax.rem(mc + d, C),
        )
        for d in range(1, C)
        for n, buf in ((1, kbuf), (2, vbuf))
    ]


def finish(a, b, c, x, y, z, sem):
    copies = [pltpu.make_async_copy(s, d, sem.at[n]) for n, (s, d) in enumerate(((a, x), (b, y), (c, z)))]
    for copy in copies:
        copy.start()
    for copy in copies:
        copy.wait()


def kernel(
    dims,
    t_ref,
    freq_ref,
    gg_ref,
    gb_ref,
    lg_ref,
    bias_ref,
    lat_hbm,
    tw_hbm,
    cw_hbm,
    qw_hbm,
    kw_hbm,
    vw_hbm,
    ow_hbm,
    sk_hbm,
    sv_hbm,
    mixed_ref,
    fk_ref,
    fv_ref,
    band,
    edges,
    halo,
    tw,
    acts,
    raw,
    cw,
    qkvw,
    ow,
    stats,
    hsend,
    hbuf,
    hfull,
    kbuf,
    vbuf,
    qown,
    qin,
    own_o,
    own_s,
    out_o,
    out_s,
    in_o,
    in_s,
    attn,
    load_sem,
    row_send,
    row_recv,
    col_send,
    col_recv,
    edge_send,
    edge_recv,
    fwd_send,
    fwd_recv,
    x_send,
    x_recv,
):
    R, C, NX, rows, cols, channels, inner, count_all = dims
    span = rows * cols
    wide = channels // R
    nb = 2
    me = lax.axis_index("row")
    mc = lax.axis_index("col")

    def remote(src, dst, send, recv, **where):
        return pltpu.make_async_remote_copy(
            src_ref=src, dst_ref=dst, send_sem=send, recv_sem=recv, device_id=where, device_id_type=MESH
        )

    loads = [
        pltpu.make_async_copy(cw_hbm, cw, load_sem.at[0]),
        pltpu.make_async_copy(qw_hbm, qkvw.at[:, 0:inner], load_sem.at[1]),
        pltpu.make_async_copy(kw_hbm, qkvw.at[:, inner : 2 * inner], load_sem.at[2]),
        pltpu.make_async_copy(vw_hbm, qkvw.at[:, 2 * inner : 3 * inner], load_sem.at[3]),
        pltpu.make_async_copy(ow_hbm, ow, load_sem.at[4]),
        pltpu.make_async_copy(sk_hbm, kbuf.at[:, 0:span], load_sem.at[5]),
        pltpu.make_async_copy(sv_hbm, vbuf.at[:, 0:span], load_sem.at[6]),
        pltpu.make_async_copy(tw_hbm, tw, load_sem.at[7]),
    ]
    own_load = pltpu.make_async_copy(lat_hbm, band.at[me], load_sem.at[8])
    own_load.start()

    barrier = pltpu.get_barrier_semaphore()
    for d in range(1, R):
        pl.semaphore_signal(barrier, inc=1, device_id={"row": lax.rem(me + d, R)}, device_id_type=MESH)
    for d in range(1, C):
        pl.semaphore_signal(barrier, inc=1, device_id={"col": lax.rem(mc + d, C)}, device_id_type=MESH)
    for n in (5, 6, 7, 0, 1, 2, 3, 4):
        loads[n].start()
    own_load.wait()
    for b in range(nb):
        x = band[me, b].astype(F32)
        edges[0, b] = x[:, cols - 1 :, :]
        edges[1, b] = x[:, 0:1, :]
    mate = me + 1 - 2 * lax.rem(me, PAIR)
    started = []

    def go(src, dst, send, recv, **where):
        copy = remote(src, dst, send, recv, **where)
        copy.start()
        started.append(copy)
        return copy

    pl.semaphore_wait(barrier, R - 1 + C - 1)

    to_right = remote(edges.at[0], halo.at[me, 0], edge_send.at[0], edge_recv.at[0], col=lax.rem(mc + 1, C))
    to_left = remote(edges.at[1], halo.at[me, 1], edge_send.at[1], edge_recv.at[1], col=lax.rem(mc + C - 1, C))

    @pl.when(mc < C - 1)
    def _():
        to_right.start()

    @pl.when(mc > 0)
    def _():
        to_left.start()

    def spread(ref, n):
        cross = [
            go(ref, ref, row_send.at[n, k], row_recv.at[n, k], row=lax.rem(me + k * PAIR, R)) for k in range(1, NX)
        ]
        return [go(ref, ref, row_send.at[n, 0], row_recv.at[n, 0], row=mate)], cross

    def relay(cross, at, n):
        handed = []
        for k in range(1, NX):
            cross[k - 1].wait_recv()
            ref = at(lax.rem(me + R - k * PAIR, R))
            handed.append(go(ref, ref, row_send.at[n, NX - 1 + k], row_recv.at[n, NX - 1 + k], row=mate))
        return handed

    lat_out = [spread(band.at[me, b], b) for b in range(nb)]
    if EARLY:
        loads[5].wait()
        loads[6].wait()
        stale_out = send_stale(go, kbuf, vbuf, span, C, mc, col_send, col_recv)

    @pl.when(mc == 0)
    def _():
        halo[me, 0] = jnp.zeros(halo.shape[2:], F32)

    @pl.when(mc == C - 1)
    def _():
        halo[me, 1] = jnp.zeros(halo.shape[2:], F32)

    @pl.when(mc > 0)
    def _():
        to_right.wait_recv()

    @pl.when(mc < C - 1)
    def _():
        to_left.wait_recv()

    halo_out = spread(halo.at[me], nb)

    half_t = freq_ref.shape[1]
    line = lax.broadcasted_iota(jnp.int32, (nb * cols, half_t), 0)
    when = jnp.where(line < cols, t_ref[0], t_ref[1]).astype(F32)
    angles = when * freq_ref[...]
    loads[7].wait()
    temb = jnp.dot(
        jax.nn.silu(jnp.cos(angles)).astype(BF16), tw[0:half_t, :], preferred_element_type=F32
    ) + jnp.dot(jax.nn.silu(jnp.sin(angles)).astype(BF16), tw[half_t:, :], preferred_element_type=F32)
    temb = temb + bias_ref[...].reshape(1, channels)
    tb = temb[:, 0:wide]
    for r in range(1, R):
        tb = jnp.where(me == r, temb[:, r * wide : (r + 1) * wide], tb)

    handed = []
    for b in range(nb):
        handed += relay(lat_out[b][1], lambda p, b=b: band.at[p, b], b)
    for b in range(nb):
        lat_out[b][0][0].wait_recv()
    for copy in handed:
        copy.wait_recv()

    one = [jnp.zeros((cols, channels), F32) for _ in range(nb)]
    two = [jnp.zeros((cols, channels), F32) for _ in range(nb)]
    for r in range(R):
        halves = []
        for b in range(nb):
            x = band[r, b].astype(F32)
            one[b] = one[b] + jnp.sum(x, axis=0)
            two[b] = two[b] + jnp.sum(x * x, axis=0)
            halves.append(x)
        raw[r * rows : (r + 1) * rows] = jnp.concatenate(halves, axis=1).astype(BF16)
    rows_of = [jnp.sum(x, axis=0, keepdims=True) for x in one + two]
    stats[0] = jnp.concatenate(rows_of + rows_of, axis=0)
    stat_out = [
        go(stats.at[0], stats.at[C - d], col_send.at[0, d], col_recv.at[0, d], col=lax.rem(mc + d, C))
        for d in range(1, C)
    ]
    handed = relay(halo_out[1], lambda p: halo.at[p], nb)
    if not EARLY:
        loads[5].wait()
        loads[6].wait()
        stale_out = send_stale(go, kbuf, vbuf, span, C, mc, col_send, col_recv)
    pick = (
        lax.broadcasted_iota(jnp.int32, (channels, wide), 0)
        == lax.broadcasted_iota(jnp.int32, (channels, wide), 1) + me * wide
    )
    acc = jnp.dot(
        raw[...].reshape(R * rows * nb * cols, channels),
        jnp.where(pick, 1.0, 0.0).astype(BF16),
        preferred_element_type=F32,
    )
    for copy in stat_out:
        copy.wait_recv()
    total = stats[0]
    for d in range(1, C):
        total = total + stats[d]
    total = group_total(total, channels // GROUPS) * (1.0 / count_all)
    mean = [total[b : b + 1] for b in range(nb)]
    scale = [lax.rsqrt(total[nb + b : nb + b + 1] - mean[b] * mean[b] + 1e-05) * gg_ref[...].reshape(1, channels) for b in range(nb)]
    bias = gb_ref[...].reshape(1, channels)

    def activate(x, b):
        y = (x - mean[b]) * scale[b] + bias
        return y * jax.nn.sigmoid(y)

    for copy in halo_out[0] + handed:
        copy.wait_recv()
    place = lax.broadcasted_iota(jnp.int32, (rows, cols, channels), 1)
    for t in range(3):
        acts[t, 0] = jnp.zeros(acts.shape[2:], BF16)
        acts[t, R * rows + 1] = jnp.zeros(acts.shape[2:], BF16)
    for r in range(R):
        tap = [[], [], []]
        for b in range(nb):
            a = activate(band[r, b].astype(F32), b)
            left = jnp.where(mc > 0, activate(halo[r, 0, b], b), 0.0)
            right = jnp.where(mc < C - 1, activate(halo[r, 1, b], b), 0.0)
            tap[0].append(jnp.where(place == 0, left, pltpu.roll(a, 1, 1)))
            tap[1].append(a)
            tap[2].append(jnp.where(place == cols - 1, right, pltpu.roll(a, cols - 1, 1)))
        for t in range(3):
            acts[t, 1 + r * rows : 1 + (r + 1) * rows] = jnp.concatenate(tap[t], axis=1).astype(BF16)
    loads[0].wait()
    for across in range(3):
        for down in range(3):
            acc = acc + lax.dot_general(
                acts[across, down : down + R * rows].reshape(R * rows * nb * cols, channels),
                cw[down, across],
                (((1,), (1,)), ((), ())),
                preferred_element_type=F32,
            )
    hid = acc.reshape(R * rows, nb * cols, wide) + tb[None]
    hsend[...] = hid.reshape(R, nb * span, wide).astype(BF16)
    h_out = []
    for d in range(1, R):
        to = lax.rem(me + d, R)
        h_out.append(go(hsend.at[to], hbuf.at[me], row_send.at[nb + 1, d], row_recv.at[nb + 1, d], row=to))
    hbuf[me] = hsend[me]
    for copy in stale_out:
        copy.wait_recv()
    forwards = [
        go(buf.at[:, 0 : C * span], buf.at[:, C * span : 2 * C * span], fwd_send.at[n], fwd_recv.at[n], row=mate)
        for n, buf in enumerate((kbuf, vbuf))
    ]
    for copy in h_out:
        copy.wait_recv()
    h = jnp.concatenate([hbuf[r].astype(F32) for r in range(R)], axis=1)
    hfull[...] = h
    centre = h - jnp.mean(h, axis=1, keepdims=True)
    spread = jnp.mean(centre * centre, axis=1, keepdims=True)
    normed = (centre * lax.rsqrt(spread + 1e-05) * lg_ref[...].reshape(1, channels)).astype(BF16)
    for n in (1, 2, 3):
        loads[n].wait()
    qkv = jnp.dot(normed, qkvw[...], preferred_element_type=F32).reshape(rows, nb, cols, 3 * inner)
    for b in range(nb):
        part = qkv[:, b].reshape(span, 3 * inner)
        qown[b] = (part[:, 0:inner] * (1.0 / HD**0.5)).astype(BF16)
        k = part[:, inner : 2 * inner].astype(BF16)
        v = part[:, 2 * inner :].astype(BF16)
        kbuf[b, 2 * C * span :] = k
        vbuf[b, 2 * C * span :] = v
        fk_ref[b] = k
        fv_ref[b] = v
    q_out = [
        go(qown, qin.at[NX - d], x_send.at[0, d], x_recv.at[0, d], row=lax.rem(me + d * PAIR, R))
        for d in range(1, NX)
    ]
    for copy in forwards:
        copy.wait_recv()

    half = lax.broadcasted_iota(jnp.int32, (span, 2 * HD), 1) < HD
    lanes = lax.broadcasted_iota(jnp.int32, (span, 128), 1)
    zero = jnp.zeros((span, 2 * HD), BF16)

    def attend(q, b, start, o_store):
        held = jnp.zeros((span, 128), F32)
        for pair in range(inner // (2 * HD)):
            at = slice(pair * 2 * HD, (pair + 1) * 2 * HD)
            q2 = q[:, at]
            q2 = jnp.concatenate([jnp.where(half, q2, zero), jnp.where(half, zero, q2)], axis=0)
            s = lax.dot_general(
                q2, kbuf[b, start : start + 2 * C * span, at], (((1,), (1,)), ((), ())), preferred_element_type=F32
            )
            m = jnp.max(s, axis=1, keepdims=True)
            p = jnp.exp(s - m)
            l = jnp.sum(p, axis=1, keepdims=True)
            o = jnp.dot(p.astype(BF16), vbuf[b, start : start + 2 * C * span, at], preferred_element_type=F32)
            o_store(at, jnp.where(half, o[:span], o[span:]))
            for n in range(2):
                held = jnp.where(lanes == pair * 2 + n, m[n * span : (n + 1) * span], held)
                held = jnp.where(lanes == 64 + pair * 2 + n, l[n * span : (n + 1) * span], held)
        return held

    for b in range(nb):

        def keep(at, o, b=b):
            own_o[b, :, at] = o

        own_s[b] = attend(qown[b], b, span, keep)

    back = []
    for d in range(1, NX):
        q_out[NX - 1 - d].wait_recv()
        for b in range(nb):

            def give(at, o, b=b, d=d):
                out_o[d, b, :, at] = o.astype(BF16)

            out_s[d, b] = attend(qin[d, b], b, 0, give)
        to = lax.rem(me + d * PAIR, R)
        for n, src, dst in ((1, out_o, in_o), (2, out_s, in_s)):
            back.append(go(src.at[d], dst.at[NX - d], x_send.at[n, d], x_recv.at[n, d], row=to))
    for copy in back:
        copy.wait_recv()
    loads[4].wait()
    for b in range(nb):
        for pair in range(inner // (2 * HD)):
            at = slice(pair * 2 * HD, (pair + 1) * 2 * HD)

            def spread_of(held, base):
                one_of = held[:, base + pair * 2 : base + pair * 2 + 1]
                two_of = held[:, base + pair * 2 + 1 : base + pair * 2 + 2]
                return jnp.where(half, one_of, two_of)

            helds = [own_s[b]] + [in_s[d, b] for d in range(1, NX)]
            sums = [own_o[b, :, at]] + [in_o[d, b, :, at].astype(F32) for d in range(1, NX)]
            peaks = [spread_of(held, 0) for held in helds]
            top = functools.reduce(jnp.maximum, peaks)
            num, den = 0.0, 0.0
            for held, o, peak in zip(helds, sums, peaks):
                factor = jnp.exp(peak - top)
                num = num + o * factor
                den = den + spread_of(held, 64) * factor
            attn[b, :, at] = (num / den).astype(BF16)
        hb = hfull[...].reshape(rows, nb, cols, channels)[:, b].reshape(span, channels)
        mixed_ref[b] = (hb + jnp.dot(attn[b], ow[...], preferred_element_type=F32)).astype(BF16)

    @pl.when(mc < C - 1)
    def _():
        to_right.wait_send()

    @pl.when(mc > 0)
    def _():
        to_left.wait_send()

    for copy in started:
        copy.wait_send()


def body(
    latent,
    timestep,
    gn_gain,
    gn_bias,
    conv_weight,
    conv_bias,
    time_weight,
    ln_gain,
    q_weight,
    k_weight,
    v_weight,
    out_weight,
    stale_keys,
    stale_values,
):
    batch, rows, cols, channels = latent.shape
    inner = q_weight.shape[1]
    R, C = lax.axis_size("row"), lax.axis_size("col")
    NX = R // PAIR
    span = rows * cols
    wide = conv_weight.shape[3]
    count_all = span * R * C * (channels // GROUPS)
    half = time_weight.shape[0] // 2
    freqs = jnp.exp(-jnp.log(10000.0) * jnp.arange(half, dtype=F32) / half).reshape(1, half)
    vm = pl.BlockSpec(memory_space=pltpu.VMEM)
    hbm = pl.BlockSpec(memory_space=pl.ANY)
    dma = pltpu.SemaphoreType.DMA
    mixed, fresh_k, fresh_v = pl.pallas_call(
        functools.partial(kernel, (R, C, NX, rows, cols, channels, inner, count_all)),
        out_shape=(
            jax.ShapeDtypeStruct((batch, span, channels), BF16),
            jax.ShapeDtypeStruct((batch, span, inner), BF16),
            jax.ShapeDtypeStruct((batch, span, inner), BF16),
        ),
        in_specs=[pl.BlockSpec(memory_space=pltpu.SMEM)] + [vm] * 5 + [hbm] * 9,
        out_specs=(vm, vm, vm),
        scratch_shapes=[
            pltpu.VMEM((R, batch, rows, cols, channels), BF16),
            pltpu.VMEM((2, batch, rows, 1, channels), F32),
            pltpu.VMEM((R, 2, batch, rows, 1, channels), F32),
            pltpu.VMEM(time_weight.shape, BF16),
            pltpu.VMEM((3, R * rows + 2, batch * cols, channels), BF16),
            pltpu.VMEM((R * rows, batch * cols, channels), BF16),
            pltpu.VMEM((3, 3, wide, channels), BF16),
            pltpu.VMEM((channels, 3 * inner), BF16),
            pltpu.VMEM((inner, channels), BF16),
            pltpu.VMEM((C, 8, channels), F32),
            pltpu.VMEM((R, batch * span, wide), BF16),
            pltpu.VMEM((R, batch * span, wide), BF16),
            pltpu.VMEM((batch * span, channels), F32),
            pltpu.VMEM((batch, (2 * C + 1) * span, inner), BF16),
            pltpu.VMEM((batch, (2 * C + 1) * span, inner), BF16),
            pltpu.VMEM((batch, span, inner), BF16),
            pltpu.VMEM((NX, batch, span, inner), BF16),
            pltpu.VMEM((batch, span, inner), F32),
            pltpu.VMEM((batch, span, 128), F32),
            pltpu.VMEM((NX, batch, span, inner), BF16),
            pltpu.VMEM((NX, batch, span, 128), F32),
            pltpu.VMEM((NX, batch, span, inner), BF16),
            pltpu.VMEM((NX, batch, span, 128), F32),
            pltpu.VMEM((batch, span, inner), BF16),
            dma((9,)),
            dma((batch + 2, R)),
            dma((batch + 2, R)),
            dma((3, C)),
            dma((3, C)),
            dma((2,)),
            dma((2,)),
            dma((2,)),
            dma((2,)),
            dma((3, NX)),
            dma((3, NX)),
        ],
        compiler_params=pltpu.CompilerParams(
            collective_id=0, has_side_effects=True, vmem_limit_bytes=56 * 1024 * 1024
        ),
    )(
        timestep,
        freqs,
        gn_gain,
        gn_bias,
        ln_gain,
        conv_bias,
        latent,
        time_weight,
        conv_weight.transpose(0, 1, 3, 2),
        q_weight,
        k_weight,
        v_weight,
        out_weight,
        stale_keys.reshape(batch, span, inner),
        stale_values.reshape(batch, span, inner),
    )
    mixed, fresh_k, fresh_v = pl.pallas_call(
        finish,
        out_shape=tuple(jax.ShapeDtypeStruct(x.shape, x.dtype) for x in (mixed, fresh_k, fresh_v)),
        in_specs=[hbm] * 3,
        out_specs=(hbm,) * 3,
        scratch_shapes=[dma((3,))],
    )(mixed, fresh_k, fresh_v)
    return (
        mixed.reshape(batch, rows, cols, channels),
        fresh_k.reshape(batch, rows, cols, inner),
        fresh_v.reshape(batch, rows, cols, inner),
    )


def solution(mesh):
    placed = (
        P("parts", "row", "col", None),
        P("parts"),
        P(),
        P(),
        P(None, None, None, "row"),
        P(),
        P(),
        P(),
        P(),
        P(),
        P(),
        P(),
        P("parts", "row", "col", None),
        P("parts", "row", "col", None),
    )
    return jax.shard_map(
        body,
        mesh=mesh,
        in_specs=placed,
        out_specs=(
            P("parts", "row", "col", None),
            P("parts", "row", "col", None),
            P("parts", "row", "col", None),
        ),
        check_vma=False,
    )
```

```python
import functools

import jax
import jax.numpy as jnp
from jax import lax
from jax.experimental import pallas as pl
from jax.experimental.pallas import tpu as pltpu
from jax.sharding import PartitionSpec as P

HD = 64
GROUPS = 32
PAIR = 2
EARLY = False
MESH = pl.DeviceIdType.MESH
F32 = jnp.float32
BF16 = jnp.bfloat16


def group_total(sums, size):
    width = sums.shape[1]
    lane = lax.broadcasted_iota(jnp.int32, sums.shape, 1)

    def window(x, sign):
        parts, total, offset = {1: x}, None, 0
        step = 1
        while step * 2 <= size:
            last = parts[step]
            parts[step * 2] = last + pltpu.roll(last, (sign * step) % width, 1)
            step *= 2
        for step in sorted(parts, reverse=True):
            if size & step:
                piece = parts[step]
                if offset:
                    piece = pltpu.roll(piece, (sign * offset) % width, 1)
                total = piece if total is None else total + piece
                offset += step
        return total

    ends = jnp.where(lax.rem(lane, size) == size - 1, window(sums, 1), 0.0)
    return window(ends, -1)


def send_stale(go, kbuf, vbuf, span, C, mc, col_send, col_recv):
    return [
        go(
            buf.at[:, 0:span],
            buf.at[:, (C - d) * span : (C - d + 1) * span],
            col_send.at[n, d],
            col_recv.at[n, d],
            col=lax.rem(mc + d, C),
        )
        for d in range(1, C)
        for n, buf in ((1, kbuf), (2, vbuf))
    ]


def finish(a, b, c, x, y, z):
    x[...] = a[...]
    y[...] = b[...]
    z[...] = c[...]


def kernel(
    dims,
    t_ref,
    freq_ref,
    gg_ref,
    gb_ref,
    lg_ref,
    bias_ref,
    lat_hbm,
    tw_hbm,
    cw_hbm,
    qw_hbm,
    kw_hbm,
    vw_hbm,
    ow_hbm,
    sk_hbm,
    sv_hbm,
    mixed_ref,
    fk_ref,
    fv_ref,
    band,
    edges,
    halo,
    tw,
    acts,
    raw,
    cw,
    qkvw,
    ow,
    stats,
    hsend,
    hbuf,
    hfull,
    kbuf,
    vbuf,
    qown,
    qin,
    own_o,
    own_s,
    out_o,
    out_s,
    in_o,
    in_s,
    attn,
    load_sem,
    row_send,
    row_recv,
    col_send,
    col_recv,
    edge_send,
    edge_recv,
    fwd_send,
    fwd_recv,
    x_send,
    x_recv,
):
    R, C, NX, rows, cols, channels, inner, count_all = dims
    span = rows * cols
    wide = channels // R
    nb = 2
    me = lax.axis_index("row")
    mc = lax.axis_index("col")

    def remote(src, dst, send, recv, **where):
        return pltpu.make_async_remote_copy(
            src_ref=src, dst_ref=dst, send_sem=send, recv_sem=recv, device_id=where, device_id_type=MESH
        )

    loads = [
        pltpu.make_async_copy(cw_hbm, cw, load_sem.at[0]),
        pltpu.make_async_copy(qw_hbm, qkvw.at[:, 0:inner], load_sem.at[1]),
        pltpu.make_async_copy(kw_hbm, qkvw.at[:, inner : 2 * inner], load_sem.at[2]),
        pltpu.make_async_copy(vw_hbm, qkvw.at[:, 2 * inner : 3 * inner], load_sem.at[3]),
        pltpu.make_async_copy(ow_hbm, ow, load_sem.at[4]),
        pltpu.make_async_copy(sk_hbm, kbuf.at[:, 0:span], load_sem.at[5]),
        pltpu.make_async_copy(sv_hbm, vbuf.at[:, 0:span], load_sem.at[6]),
        pltpu.make_async_copy(tw_hbm, tw, load_sem.at[7]),
    ]
    own_load = pltpu.make_async_copy(lat_hbm, band.at[me], load_sem.at[8])
    own_load.start()

    barrier = pltpu.get_barrier_semaphore()
    for d in range(1, R):
        pl.semaphore_signal(barrier, inc=1, device_id={"row": lax.rem(me + d, R)}, device_id_type=MESH)
    for d in range(1, C):
        pl.semaphore_signal(barrier, inc=1, device_id={"col": lax.rem(mc + d, C)}, device_id_type=MESH)
    for n in (5, 6, 7, 0, 1, 2, 3, 4):
        loads[n].start()
    own_load.wait()
    for b in range(nb):
        x = band[me, b].astype(F32)
        edges[0, b] = x[:, cols - 1 :, :]
        edges[1, b] = x[:, 0:1, :]
    mate = me + 1 - 2 * lax.rem(me, PAIR)
    started = []

    def go(src, dst, send, recv, **where):
        copy = remote(src, dst, send, recv, **where)
        copy.start()
        started.append(copy)
        return copy

    pl.semaphore_wait(barrier, R - 1 + C - 1)

    to_right = remote(edges.at[0], halo.at[me, 0], edge_send.at[0], edge_recv.at[0], col=lax.rem(mc + 1, C))
    to_left = remote(edges.at[1], halo.at[me, 1], edge_send.at[1], edge_recv.at[1], col=lax.rem(mc + C - 1, C))

    @pl.when(mc < C - 1)
    def _():
        to_right.start()

    @pl.when(mc > 0)
    def _():
        to_left.start()

    def spread(ref, n):
        cross = [
            go(ref, ref, row_send.at[n, k], row_recv.at[n, k], row=lax.rem(me + k * PAIR, R)) for k in range(1, NX)
        ]
        return [go(ref, ref, row_send.at[n, 0], row_recv.at[n, 0], row=mate)], cross

    def relay(cross, at, n):
        handed = []
        for k in range(1, NX):
            cross[k - 1].wait_recv()
            ref = at(lax.rem(me + R - k * PAIR, R))
            handed.append(go(ref, ref, row_send.at[n, NX - 1 + k], row_recv.at[n, NX - 1 + k], row=mate))
        return handed

    lat_out = [spread(band.at[me, b], b) for b in range(nb)]
    if EARLY:
        loads[5].wait()
        loads[6].wait()
        stale_out = send_stale(go, kbuf, vbuf, span, C, mc, col_send, col_recv)

    @pl.when(mc == 0)
    def _():
        halo[me, 0] = jnp.zeros(halo.shape[2:], F32)

    @pl.when(mc == C - 1)
    def _():
        halo[me, 1] = jnp.zeros(halo.shape[2:], F32)

    @pl.when(mc > 0)
    def _():
        to_right.wait_recv()

    @pl.when(mc < C - 1)
    def _():
        to_left.wait_recv()

    halo_out = spread(halo.at[me], nb)

    half_t = freq_ref.shape[1]
    line = lax.broadcasted_iota(jnp.int32, (nb * cols, half_t), 0)
    when = jnp.where(line < cols, t_ref[0], t_ref[1]).astype(F32)
    angles = when * freq_ref[...]
    loads[7].wait()
    temb = jnp.dot(
        jax.nn.silu(jnp.cos(angles)).astype(BF16), tw[0:half_t, :], preferred_element_type=F32
    ) + jnp.dot(jax.nn.silu(jnp.sin(angles)).astype(BF16), tw[half_t:, :], preferred_element_type=F32)
    temb = temb + bias_ref[...].reshape(1, channels)
    tb = temb[:, 0:wide]
    for r in range(1, R):
        tb = jnp.where(me == r, temb[:, r * wide : (r + 1) * wide], tb)

    handed = []
    for b in range(nb):
        handed += relay(lat_out[b][1], lambda p, b=b: band.at[p, b], b)
    for b in range(nb):
        lat_out[b][0][0].wait_recv()
    for copy in handed:
        copy.wait_recv()

    one = [jnp.zeros((cols, channels), F32) for _ in range(nb)]
    two = [jnp.zeros((cols, channels), F32) for _ in range(nb)]
    for r in range(R):
        halves = []
        for b in range(nb):
            x = band[r, b].astype(F32)
            one[b] = one[b] + jnp.sum(x, axis=0)
            two[b] = two[b] + jnp.sum(x * x, axis=0)
            halves.append(x)
        raw[r * rows : (r + 1) * rows] = jnp.concatenate(halves, axis=1).astype(BF16)
    rows_of = [jnp.sum(x, axis=0, keepdims=True) for x in one + two]
    stats[0] = jnp.concatenate(rows_of + rows_of, axis=0)
    stat_out = [
        go(stats.at[0], stats.at[C - d], col_send.at[0, d], col_recv.at[0, d], col=lax.rem(mc + d, C))
        for d in range(1, C)
    ]
    handed = relay(halo_out[1], lambda p: halo.at[p], nb)
    if not EARLY:
        loads[5].wait()
        loads[6].wait()
        stale_out = send_stale(go, kbuf, vbuf, span, C, mc, col_send, col_recv)
    pick = (
        lax.broadcasted_iota(jnp.int32, (channels, wide), 0)
        == lax.broadcasted_iota(jnp.int32, (channels, wide), 1) + me * wide
    )
    acc = jnp.dot(
        raw[...].reshape(R * rows * nb * cols, channels),
        jnp.where(pick, 1.0, 0.0).astype(BF16),
        preferred_element_type=F32,
    )
    for copy in stat_out:
        copy.wait_recv()
    total = stats[0]
    for d in range(1, C):
        total = total + stats[d]
    total = group_total(total, channels // GROUPS) * (1.0 / count_all)
    mean = [total[b : b + 1] for b in range(nb)]
    scale = [lax.rsqrt(total[nb + b : nb + b + 1] - mean[b] * mean[b] + 1e-05) * gg_ref[...].reshape(1, channels) for b in range(nb)]
    bias = gb_ref[...].reshape(1, channels)

    def activate(x, b):
        y = (x - mean[b]) * scale[b] + bias
        return y * jax.nn.sigmoid(y)

    for copy in halo_out[0] + handed:
        copy.wait_recv()
    place = lax.broadcasted_iota(jnp.int32, (rows, cols, channels), 1)
    for t in range(3):
        acts[t, 0] = jnp.zeros(acts.shape[2:], BF16)
        acts[t, R * rows + 1] = jnp.zeros(acts.shape[2:], BF16)
    for r in range(R):
        tap = [[], [], []]
        for b in range(nb):
            a = activate(band[r, b].astype(F32), b)
            left = jnp.where(mc > 0, activate(halo[r, 0, b], b), 0.0)
            right = jnp.where(mc < C - 1, activate(halo[r, 1, b], b), 0.0)
            tap[0].append(jnp.where(place == 0, left, pltpu.roll(a, 1, 1)))
            tap[1].append(a)
            tap[2].append(jnp.where(place == cols - 1, right, pltpu.roll(a, cols - 1, 1)))
        for t in range(3):
            acts[t, 1 + r * rows : 1 + (r + 1) * rows] = jnp.concatenate(tap[t], axis=1).astype(BF16)
    loads[0].wait()
    for across in range(3):
        for down in range(3):
            acc = acc + lax.dot_general(
                acts[across, down : down + R * rows].reshape(R * rows * nb * cols, channels),
                cw[down, across],
                (((1,), (1,)), ((), ())),
                preferred_element_type=F32,
            )
    hid = acc.reshape(R * rows, nb * cols, wide) + tb[None]
    hsend[...] = hid.reshape(R, nb * span, wide).astype(BF16)
    h_out = []
    for d in range(1, R):
        to = lax.rem(me + d, R)
        h_out.append(go(hsend.at[to], hbuf.at[me], row_send.at[nb + 1, d], row_recv.at[nb + 1, d], row=to))
    hbuf[me] = hsend[me]
    for copy in stale_out:
        copy.wait_recv()
    forwards = [
        go(buf.at[:, 0 : C * span], buf.at[:, C * span : 2 * C * span], fwd_send.at[n], fwd_recv.at[n], row=mate)
        for n, buf in enumerate((kbuf, vbuf))
    ]
    for copy in h_out:
        copy.wait_recv()
    h = jnp.concatenate([hbuf[r].astype(F32) for r in range(R)], axis=1)
    hfull[...] = h
    centre = h - jnp.mean(h, axis=1, keepdims=True)
    spread = jnp.mean(centre * centre, axis=1, keepdims=True)
    normed = (centre * lax.rsqrt(spread + 1e-05) * lg_ref[...].reshape(1, channels)).astype(BF16)
    for n in (1, 2, 3):
        loads[n].wait()
    qkv = jnp.dot(normed, qkvw[...], preferred_element_type=F32).reshape(rows, nb, cols, 3 * inner)
    for b in range(nb):
        part = qkv[:, b].reshape(span, 3 * inner)
        qown[b] = (part[:, 0:inner] * (1.0 / HD**0.5)).astype(BF16)
        k = part[:, inner : 2 * inner].astype(BF16)
        v = part[:, 2 * inner :].astype(BF16)
        kbuf[b, 2 * C * span :] = k
        vbuf[b, 2 * C * span :] = v
        fk_ref[b] = k
        fv_ref[b] = v
    q_out = [
        go(qown, qin.at[NX - d], x_send.at[0, d], x_recv.at[0, d], row=lax.rem(me + d * PAIR, R))
        for d in range(1, NX)
    ]
    for copy in forwards:
        copy.wait_recv()

    half = lax.broadcasted_iota(jnp.int32, (span, 2 * HD), 1) < HD
    lanes = lax.broadcasted_iota(jnp.int32, (span, 128), 1)
    zero = jnp.zeros((span, 2 * HD), BF16)

    def attend(q, b, start, o_store):
        held = jnp.zeros((span, 128), F32)
        for pair in range(inner // (2 * HD)):
            at = slice(pair * 2 * HD, (pair + 1) * 2 * HD)
            q2 = q[:, at]
            q2 = jnp.concatenate([jnp.where(half, q2, zero), jnp.where(half, zero, q2)], axis=0)
            s = lax.dot_general(
                q2, kbuf[b, start : start + 2 * C * span, at], (((1,), (1,)), ((), ())), preferred_element_type=F32
            )
            m = jnp.max(s, axis=1, keepdims=True)
            p = jnp.exp(s - m)
            l = jnp.sum(p, axis=1, keepdims=True)
            o = jnp.dot(p.astype(BF16), vbuf[b, start : start + 2 * C * span, at], preferred_element_type=F32)
            o_store(at, jnp.where(half, o[:span], o[span:]))
            for n in range(2):
                held = jnp.where(lanes == pair * 2 + n, m[n * span : (n + 1) * span], held)
                held = jnp.where(lanes == 64 + pair * 2 + n, l[n * span : (n + 1) * span], held)
        return held

    for b in range(nb):

        def keep(at, o, b=b):
            own_o[b, :, at] = o

        own_s[b] = attend(qown[b], b, span, keep)

    back = []
    for d in range(1, NX):
        q_out[NX - 1 - d].wait_recv()
        for b in range(nb):

            def give(at, o, b=b, d=d):
                out_o[d, b, :, at] = o.astype(BF16)

            out_s[d, b] = attend(qin[d, b], b, 0, give)
        to = lax.rem(me + d * PAIR, R)
        for n, src, dst in ((1, out_o, in_o), (2, out_s, in_s)):
            back.append(go(src.at[d], dst.at[NX - d], x_send.at[n, d], x_recv.at[n, d], row=to))
    for copy in back:
        copy.wait_recv()
    loads[4].wait()
    for b in range(nb):
        for pair in range(inner // (2 * HD)):
            at = slice(pair * 2 * HD, (pair + 1) * 2 * HD)

            def spread_of(held, base):
                one_of = held[:, base + pair * 2 : base + pair * 2 + 1]
                two_of = held[:, base + pair * 2 + 1 : base + pair * 2 + 2]
                return jnp.where(half, one_of, two_of)

            helds = [own_s[b]] + [in_s[d, b] for d in range(1, NX)]
            sums = [own_o[b, :, at]] + [in_o[d, b, :, at].astype(F32) for d in range(1, NX)]
            peaks = [spread_of(held, 0) for held in helds]
            top = functools.reduce(jnp.maximum, peaks)
            num, den = 0.0, 0.0
            for held, o, peak in zip(helds, sums, peaks):
                factor = jnp.exp(peak - top)
                num = num + o * factor
                den = den + spread_of(held, 64) * factor
            attn[b, :, at] = (num / den).astype(BF16)
        hb = hfull[...].reshape(rows, nb, cols, channels)[:, b].reshape(span, channels)
        mixed_ref[b] = (hb + jnp.dot(attn[b], ow[...], preferred_element_type=F32)).astype(BF16)

    @pl.when(mc < C - 1)
    def _():
        to_right.wait_send()

    @pl.when(mc > 0)
    def _():
        to_left.wait_send()

    for copy in started:
        copy.wait_send()


def body(
    latent,
    timestep,
    gn_gain,
    gn_bias,
    conv_weight,
    conv_bias,
    time_weight,
    ln_gain,
    q_weight,
    k_weight,
    v_weight,
    out_weight,
    stale_keys,
    stale_values,
):
    batch, rows, cols, channels = latent.shape
    inner = q_weight.shape[1]
    R, C = lax.axis_size("row"), lax.axis_size("col")
    NX = R // PAIR
    span = rows * cols
    wide = conv_weight.shape[3]
    count_all = span * R * C * (channels // GROUPS)
    half = time_weight.shape[0] // 2
    freqs = jnp.exp(-jnp.log(10000.0) * jnp.arange(half, dtype=F32) / half).reshape(1, half)
    vm = pl.BlockSpec(memory_space=pltpu.VMEM)
    hbm = pl.BlockSpec(memory_space=pl.ANY)
    dma = pltpu.SemaphoreType.DMA
    mixed, fresh_k, fresh_v = pl.pallas_call(
        functools.partial(kernel, (R, C, NX, rows, cols, channels, inner, count_all)),
        out_shape=(
            jax.ShapeDtypeStruct((batch, span, channels), BF16),
            jax.ShapeDtypeStruct((batch, span, inner), BF16),
            jax.ShapeDtypeStruct((batch, span, inner), BF16),
        ),
        in_specs=[pl.BlockSpec(memory_space=pltpu.SMEM)] + [vm] * 5 + [hbm] * 9,
        out_specs=(vm, vm, vm),
        scratch_shapes=[
            pltpu.VMEM((R, batch, rows, cols, channels), BF16),
            pltpu.VMEM((2, batch, rows, 1, channels), F32),
            pltpu.VMEM((R, 2, batch, rows, 1, channels), F32),
            pltpu.VMEM(time_weight.shape, BF16),
            pltpu.VMEM((3, R * rows + 2, batch * cols, channels), BF16),
            pltpu.VMEM((R * rows, batch * cols, channels), BF16),
            pltpu.VMEM((3, 3, wide, channels), BF16),
            pltpu.VMEM((channels, 3 * inner), BF16),
            pltpu.VMEM((inner, channels), BF16),
            pltpu.VMEM((C, 8, channels), F32),
            pltpu.VMEM((R, batch * span, wide), BF16),
            pltpu.VMEM((R, batch * span, wide), BF16),
            pltpu.VMEM((batch * span, channels), F32),
            pltpu.VMEM((batch, (2 * C + 1) * span, inner), BF16),
            pltpu.VMEM((batch, (2 * C + 1) * span, inner), BF16),
            pltpu.VMEM((batch, span, inner), BF16),
            pltpu.VMEM((NX, batch, span, inner), BF16),
            pltpu.VMEM((batch, span, inner), F32),
            pltpu.VMEM((batch, span, 128), F32),
            pltpu.VMEM((NX, batch, span, inner), BF16),
            pltpu.VMEM((NX, batch, span, 128), F32),
            pltpu.VMEM((NX, batch, span, inner), BF16),
            pltpu.VMEM((NX, batch, span, 128), F32),
            pltpu.VMEM((batch, span, inner), BF16),
            dma((9,)),
            dma((batch + 2, R)),
            dma((batch + 2, R)),
            dma((3, C)),
            dma((3, C)),
            dma((2,)),
            dma((2,)),
            dma((2,)),
            dma((2,)),
            dma((3, NX)),
            dma((3, NX)),
        ],
        compiler_params=pltpu.CompilerParams(
            collective_id=0, has_side_effects=True, vmem_limit_bytes=56 * 1024 * 1024
        ),
    )(
        timestep,
        freqs,
        gn_gain,
        gn_bias,
        ln_gain,
        conv_bias,
        latent,
        time_weight,
        conv_weight.transpose(0, 1, 3, 2),
        q_weight,
        k_weight,
        v_weight,
        out_weight,
        stale_keys.reshape(batch, span, inner),
        stale_values.reshape(batch, span, inner),
    )
    mixed, fresh_k, fresh_v = pl.pallas_call(
        finish,
        out_shape=tuple(jax.ShapeDtypeStruct(x.shape, x.dtype) for x in (mixed, fresh_k, fresh_v)),
        in_specs=[vm] * 3,
        out_specs=(vm,) * 3,
    )(mixed, fresh_k, fresh_v)
    return (
        mixed.reshape(batch, rows, cols, channels),
        fresh_k.reshape(batch, rows, cols, inner),
        fresh_v.reshape(batch, rows, cols, inner),
    )


def solution(mesh):
    placed = (
        P("parts", "row", "col", None),
        P("parts"),
        P(),
        P(),
        P(None, None, None, "row"),
        P(),
        P(),
        P(),
        P(),
        P(),
        P(),
        P(),
        P("parts", "row", "col", None),
        P("parts", "row", "col", None),
    )
    return jax.shard_map(
        body,
        mesh=mesh,
        in_specs=placed,
        out_specs=(
            P("parts", "row", "col", None),
            P("parts", "row", "col", None),
            P("parts", "row", "col", None),
        ),
        check_vma=False,
    )
```

```python
import functools

import jax
import jax.numpy as jnp
from jax import lax
from jax.experimental import pallas as pl
from jax.experimental.pallas import tpu as pltpu
from jax.sharding import PartitionSpec as P

HD = 64
GROUPS = 32
PAIR = 2
MESH = pl.DeviceIdType.MESH
F32 = jnp.float32
BF16 = jnp.bfloat16


def group_total(sums, size):
    width = sums.shape[1]
    lane = lax.broadcasted_iota(jnp.int32, sums.shape, 1)

    def window(x, sign):
        parts, total, offset = {1: x}, None, 0
        step = 1
        while step * 2 <= size:
            last = parts[step]
            parts[step * 2] = last + pltpu.roll(last, (sign * step) % width, 1)
            step *= 2
        for step in sorted(parts, reverse=True):
            if size & step:
                piece = parts[step]
                if offset:
                    piece = pltpu.roll(piece, (sign * offset) % width, 1)
                total = piece if total is None else total + piece
                offset += step
        return total

    ends = jnp.where(lax.rem(lane, size) == size - 1, window(sums, 1), 0.0)
    return window(ends, -1)


def finish(a, b, c, x, y, z):
    x[...] = a[...]
    y[...] = b[...]
    z[...] = c[...]


def kernel(
    dims,
    t_ref,
    gg_ref,
    gb_ref,
    lg_ref,
    bias_ref,
    lat_hbm,
    tw_hbm,
    cw_hbm,
    qw_hbm,
    kw_hbm,
    vw_hbm,
    ow_hbm,
    sk_hbm,
    sv_hbm,
    mixed_ref,
    fk_ref,
    fv_ref,
    band,
    edges,
    halo,
    tw,
    acts,
    raw,
    cw,
    qkvw,
    ow,
    stats,
    hsend,
    hbuf,
    hfull,
    kbuf,
    vbuf,
    qown,
    qin,
    own_o,
    own_s,
    out_o,
    out_s,
    in_o,
    in_s,
    attn,
    load_sem,
    row_send,
    row_recv,
    col_send,
    col_recv,
    hop_send,
    hop_recv,
    edge_send,
    edge_recv,
    fwd_send,
    fwd_recv,
    x_send,
    x_recv,
):
    R, C, NX, rows, cols, channels, inner, count_all = dims
    span = rows * cols
    wide = channels // R
    nb = 2
    me = lax.axis_index("row")
    mc = lax.axis_index("col")

    def remote(src, dst, send, recv, **where):
        return pltpu.make_async_remote_copy(
            src_ref=src, dst_ref=dst, send_sem=send, recv_sem=recv, device_id=where, device_id_type=MESH
        )

    loads = [
        pltpu.make_async_copy(cw_hbm, cw, load_sem.at[0]),
        pltpu.make_async_copy(qw_hbm, qkvw.at[:, 0:inner], load_sem.at[1]),
        pltpu.make_async_copy(kw_hbm, qkvw.at[:, inner : 2 * inner], load_sem.at[2]),
        pltpu.make_async_copy(vw_hbm, qkvw.at[:, 2 * inner : 3 * inner], load_sem.at[3]),
        pltpu.make_async_copy(ow_hbm, ow, load_sem.at[4]),
        pltpu.make_async_copy(sk_hbm, kbuf.at[:, 0:span], load_sem.at[5]),
        pltpu.make_async_copy(sv_hbm, vbuf.at[:, 0:span], load_sem.at[6]),
        pltpu.make_async_copy(tw_hbm, tw, load_sem.at[7]),
    ]
    own_load = pltpu.make_async_copy(lat_hbm, band.at[me], load_sem.at[8])
    own_load.start()

    barrier = pltpu.get_barrier_semaphore()
    for d in range(1, R):
        pl.semaphore_signal(barrier, inc=1, device_id={"row": lax.rem(me + d, R)}, device_id_type=MESH)
    for d in range(1, C):
        pl.semaphore_signal(barrier, inc=1, device_id={"col": lax.rem(mc + d, C)}, device_id_type=MESH)
    for n in (5, 6, 7, 0, 1, 2, 3, 4):
        loads[n].start()
    own_load.wait()
    for b in range(nb):
        x = band[me, b].astype(F32)
        edges[0, b] = x[:, cols - 1 :, :]
        edges[1, b] = x[:, 0:1, :]
    mate = me + 1 - 2 * lax.rem(me, PAIR)
    started = []

    def go(src, dst, send, recv, **where):
        copy = remote(src, dst, send, recv, **where)
        copy.start()
        started.append(copy)
        return copy

    pl.semaphore_wait(barrier, R - 1 + C - 1)

    to_right = remote(edges.at[0], halo.at[me, 0], edge_send.at[0], edge_recv.at[0], col=lax.rem(mc + 1, C))
    to_left = remote(edges.at[1], halo.at[me, 1], edge_send.at[1], edge_recv.at[1], col=lax.rem(mc + C - 1, C))

    @pl.when(mc < C - 1)
    def _():
        to_right.start()

    @pl.when(mc > 0)
    def _():
        to_left.start()

    def spread(ref, n):
        cross = [
            go(ref, ref, row_send.at[n, k], row_recv.at[n, k], row=lax.rem(me + k * PAIR, R)) for k in range(1, NX)
        ]
        return [go(ref, ref, row_send.at[n, 0], row_recv.at[n, 0], row=mate)], cross

    def relay(cross, at, n):
        handed = []
        for k in range(1, NX):
            cross[k - 1].wait_recv()
            ref = at(lax.rem(me + R - k * PAIR, R))
            handed.append(go(ref, ref, row_send.at[n, NX - 1 + k], row_recv.at[n, NX - 1 + k], row=mate))
        return handed

    lat_out = [spread(band.at[me, b], b) for b in range(nb)]

    def hops(k):
        made = []
        for n, buf in enumerate((kbuf, vbuf)):
            for way, slot, dest, to, sends, takes in (
                (0, (C - k + 1) % C, C - k, mc + 1, (mc >= k - 1) & (mc < C - 1), mc >= k),
                (1, k - 1, k, mc + C - 1, (mc <= C - k) & (mc > 0), mc <= C - 1 - k),
            ):
                copy = remote(
                    buf.at[:, slot * span : (slot + 1) * span],
                    buf.at[:, dest * span : (dest + 1) * span],
                    hop_send.at[k, n, way],
                    hop_recv.at[k, n, way],
                    col=lax.rem(to, C),
                )
                made.append((copy, sends, takes))
        return made

    def each(k, act, which):
        for hop in hops(k):

            @pl.when(hop[which])
            def _(copy=hop[0]):
                act(copy)

    def send_hop(k):
        if k < C:
            if k > 1:
                each(k - 1, lambda copy: copy.wait_recv(), 2)
            each(k, lambda copy: copy.start(), 1)

    loads[5].wait()
    loads[6].wait()
    send_hop(1)

    @pl.when(mc == 0)
    def _():
        halo[me, 0] = jnp.zeros(halo.shape[2:], F32)

    @pl.when(mc == C - 1)
    def _():
        halo[me, 1] = jnp.zeros(halo.shape[2:], F32)

    @pl.when(mc > 0)
    def _():
        to_right.wait_recv()

    @pl.when(mc < C - 1)
    def _():
        to_left.wait_recv()

    halo_out = spread(halo.at[me], nb)

    half_t = tw.shape[0] // 2
    line = lax.broadcasted_iota(jnp.int32, (nb * cols, half_t), 0)
    when = jnp.where(line < cols, t_ref[0], t_ref[1]).astype(F32)
    place_t = lax.broadcasted_iota(jnp.int32, (nb * cols, half_t), 1).astype(F32)
    angles = when * jnp.exp(-jnp.log(jnp.full((1, 1), 10000.0, F32)) * place_t / half_t)
    loads[7].wait()
    temb = jnp.dot(
        jax.nn.silu(jnp.cos(angles)).astype(BF16), tw[0:half_t, :], preferred_element_type=F32
    ) + jnp.dot(jax.nn.silu(jnp.sin(angles)).astype(BF16), tw[half_t:, :], preferred_element_type=F32)
    temb = temb + bias_ref[...].reshape(1, channels)
    tb = temb[:, 0:wide]
    for r in range(1, R):
        tb = jnp.where(me == r, temb[:, r * wide : (r + 1) * wide], tb)

    handed = []
    for b in range(nb):
        handed += relay(lat_out[b][1], lambda p, b=b: band.at[p, b], b)
    for b in range(nb):
        lat_out[b][0][0].wait_recv()
    for copy in handed:
        copy.wait_recv()

    one = [jnp.zeros((cols, channels), F32) for _ in range(nb)]
    two = [jnp.zeros((cols, channels), F32) for _ in range(nb)]
    for r in range(R):
        halves = []
        for b in range(nb):
            x = band[r, b].astype(F32)
            one[b] = one[b] + jnp.sum(x, axis=0)
            two[b] = two[b] + jnp.sum(x * x, axis=0)
            halves.append(x)
        raw[r * rows : (r + 1) * rows] = jnp.concatenate(halves, axis=1).astype(BF16)
    rows_of = [jnp.sum(x, axis=0, keepdims=True) for x in one + two]
    stats[0] = jnp.concatenate(rows_of + rows_of, axis=0)
    stat_out = [
        go(stats.at[0], stats.at[C - d], col_send.at[0, d], col_recv.at[0, d], col=lax.rem(mc + d, C))
        for d in range(1, C)
    ]
    handed = relay(halo_out[1], lambda p: halo.at[p], nb)
    send_hop(2)
    pick = (
        lax.broadcasted_iota(jnp.int32, (channels, wide), 0)
        == lax.broadcasted_iota(jnp.int32, (channels, wide), 1) + me * wide
    )
    acc = jnp.dot(
        raw[...].reshape(R * rows * nb * cols, channels),
        jnp.where(pick, 1.0, 0.0).astype(BF16),
        preferred_element_type=F32,
    )
    for copy in stat_out:
        copy.wait_recv()
    total = stats[0]
    for d in range(1, C):
        total = total + stats[d]
    total = group_total(total, channels // GROUPS) * (1.0 / count_all)
    mean = [total[b : b + 1] for b in range(nb)]
    scale = [lax.rsqrt(total[nb + b : nb + b + 1] - mean[b] * mean[b] + 1e-05) * gg_ref[...].reshape(1, channels) for b in range(nb)]
    bias = gb_ref[...].reshape(1, channels)

    def activate(x, b):
        y = (x - mean[b]) * scale[b] + bias
        return y * jax.nn.sigmoid(y)

    for copy in halo_out[0] + handed:
        copy.wait_recv()
    place = lax.broadcasted_iota(jnp.int32, (rows, cols, channels), 1)
    for t in range(3):
        acts[t, 0] = jnp.zeros(acts.shape[2:], BF16)
        acts[t, R * rows + 1] = jnp.zeros(acts.shape[2:], BF16)
    for r in range(R):
        tap = [[], [], []]
        for b in range(nb):
            a = activate(band[r, b].astype(F32), b)
            left = jnp.where(mc > 0, activate(halo[r, 0, b], b), 0.0)
            right = jnp.where(mc < C - 1, activate(halo[r, 1, b], b), 0.0)
            tap[0].append(jnp.where(place == 0, left, pltpu.roll(a, 1, 1)))
            tap[1].append(a)
            tap[2].append(jnp.where(place == cols - 1, right, pltpu.roll(a, cols - 1, 1)))
        for t in range(3):
            acts[t, 1 + r * rows : 1 + (r + 1) * rows] = jnp.concatenate(tap[t], axis=1).astype(BF16)
    loads[0].wait()
    for across in range(3):
        if across:
            send_hop(across + 2)
        for down in range(3):
            acc = acc + lax.dot_general(
                acts[across, down : down + R * rows].reshape(R * rows * nb * cols, channels),
                cw[down, across],
                (((1,), (1,)), ((), ())),
                preferred_element_type=F32,
            )
    hid = acc.reshape(R * rows, nb * cols, wide) + tb[None]
    hsend[...] = hid.reshape(R, nb * span, wide).astype(BF16)
    h_out = []
    for d in range(1, R):
        to = lax.rem(me + d, R)
        h_out.append(go(hsend.at[to], hbuf.at[me], row_send.at[nb + 1, d], row_recv.at[nb + 1, d], row=to))
    hbuf[me] = hsend[me]
    for k in range(5, C + 1):
        send_hop(k)
    each(C - 1, lambda copy: copy.wait_recv(), 2)
    forwards = [
        go(buf.at[:, 0 : C * span], buf.at[:, C * span : 2 * C * span], fwd_send.at[n], fwd_recv.at[n], row=mate)
        for n, buf in enumerate((kbuf, vbuf))
    ]
    for copy in h_out:
        copy.wait_recv()
    h = jnp.concatenate([hbuf[r].astype(F32) for r in range(R)], axis=1)
    hfull[...] = h
    centre = h - jnp.mean(h, axis=1, keepdims=True)
    spread = jnp.mean(centre * centre, axis=1, keepdims=True)
    normed = (centre * lax.rsqrt(spread + 1e-05) * lg_ref[...].reshape(1, channels)).astype(BF16)
    for n in (1, 2, 3):
        loads[n].wait()
    qkv = jnp.dot(normed, qkvw[...], preferred_element_type=F32).reshape(rows, nb, cols, 3 * inner)
    for b in range(nb):
        part = qkv[:, b].reshape(span, 3 * inner)
        qown[b] = (part[:, 0:inner] * (1.0 / HD**0.5)).astype(BF16)
        k = part[:, inner : 2 * inner].astype(BF16)
        v = part[:, 2 * inner :].astype(BF16)
        kbuf[b, 2 * C * span :] = k
        vbuf[b, 2 * C * span :] = v
        fk_ref[b] = k
        fv_ref[b] = v
    q_out = [
        go(qown, qin.at[NX - d], x_send.at[0, d], x_recv.at[0, d], row=lax.rem(me + d * PAIR, R))
        for d in range(1, NX)
    ]
    for copy in forwards:
        copy.wait_recv()

    half = lax.broadcasted_iota(jnp.int32, (span, 2 * HD), 1) < HD
    lanes = lax.broadcasted_iota(jnp.int32, (span, 128), 1)
    zero = jnp.zeros((span, 2 * HD), BF16)

    def attend(q, b, start, o_store):
        held = jnp.zeros((span, 128), F32)
        for pair in range(inner // (2 * HD)):
            at = slice(pair * 2 * HD, (pair + 1) * 2 * HD)
            q2 = q[:, at]
            q2 = jnp.concatenate([jnp.where(half, q2, zero), jnp.where(half, zero, q2)], axis=0)
            s = lax.dot_general(
                q2, kbuf[b, start : start + 2 * C * span, at], (((1,), (1,)), ((), ())), preferred_element_type=F32
            )
            m = jnp.max(s, axis=1, keepdims=True)
            p = jnp.exp(s - m)
            l = jnp.sum(p, axis=1, keepdims=True)
            o = jnp.dot(p.astype(BF16), vbuf[b, start : start + 2 * C * span, at], preferred_element_type=F32)
            o_store(at, jnp.where(half, o[:span], o[span:]))
            for n in range(2):
                held = jnp.where(lanes == pair * 2 + n, m[n * span : (n + 1) * span], held)
                held = jnp.where(lanes == 64 + pair * 2 + n, l[n * span : (n + 1) * span], held)
        return held

    for b in range(nb):

        def keep(at, o, b=b):
            own_o[b, :, at] = o

        own_s[b] = attend(qown[b], b, span, keep)

    back = []
    for d in range(1, NX):
        q_out[NX - 1 - d].wait_recv()
        for b in range(nb):

            def give(at, o, b=b, d=d):
                out_o[d, b, :, at] = o.astype(BF16)

            out_s[d, b] = attend(qin[d, b], b, 0, give)
            to = lax.rem(me + d * PAIR, R)
            for n, src, dst in ((1, out_o, in_o), (3, out_s, in_s)):
                n = n + b
                back.append((b, go(src.at[d, b], dst.at[NX - d, b], x_send.at[n, d], x_recv.at[n, d], row=to)))
    loads[4].wait()
    for b in range(nb):
        for owner, copy in back:
            if owner == b:
                copy.wait_recv()
        for pair in range(inner // (2 * HD)):
            at = slice(pair * 2 * HD, (pair + 1) * 2 * HD)

            def spread_of(held, base):
                one_of = held[:, base + pair * 2 : base + pair * 2 + 1]
                two_of = held[:, base + pair * 2 + 1 : base + pair * 2 + 2]
                return jnp.where(half, one_of, two_of)

            helds = [own_s[b]] + [in_s[d, b] for d in range(1, NX)]
            sums = [own_o[b, :, at]] + [in_o[d, b, :, at].astype(F32) for d in range(1, NX)]
            peaks = [spread_of(held, 0) for held in helds]
            top = functools.reduce(jnp.maximum, peaks)
            num, den = 0.0, 0.0
            for held, o, peak in zip(helds, sums, peaks):
                factor = jnp.exp(peak - top)
                num = num + o * factor
                den = den + spread_of(held, 64) * factor
            attn[b, :, at] = (num / den).astype(BF16)
        hb = hfull[...].reshape(rows, nb, cols, channels)[:, b].reshape(span, channels)
        mixed_ref[b] = (hb + jnp.dot(attn[b], ow[...], preferred_element_type=F32)).astype(BF16)

    @pl.when(mc < C - 1)
    def _():
        to_right.wait_send()

    @pl.when(mc > 0)
    def _():
        to_left.wait_send()

    for k in range(1, C):
        each(k, lambda copy: copy.wait_send(), 1)
    for copy in started:
        copy.wait_send()


def body(
    latent,
    timestep,
    gn_gain,
    gn_bias,
    conv_weight,
    conv_bias,
    time_weight,
    ln_gain,
    q_weight,
    k_weight,
    v_weight,
    out_weight,
    stale_keys,
    stale_values,
):
    batch, rows, cols, channels = latent.shape
    inner = q_weight.shape[1]
    R, C = lax.axis_size("row"), lax.axis_size("col")
    NX = R // PAIR
    span = rows * cols
    wide = conv_weight.shape[3]
    count_all = span * R * C * (channels // GROUPS)
    vm = pl.BlockSpec(memory_space=pltpu.VMEM)
    hbm = pl.BlockSpec(memory_space=pl.ANY)
    dma = pltpu.SemaphoreType.DMA
    mixed, fresh_k, fresh_v = pl.pallas_call(
        functools.partial(kernel, (R, C, NX, rows, cols, channels, inner, count_all)),
        out_shape=(
            jax.ShapeDtypeStruct((batch, span, channels), BF16),
            jax.ShapeDtypeStruct((batch, span, inner), BF16),
            jax.ShapeDtypeStruct((batch, span, inner), BF16),
        ),
        in_specs=[pl.BlockSpec(memory_space=pltpu.SMEM)] + [vm] * 4 + [hbm] * 9,
        out_specs=(vm, vm, vm),
        scratch_shapes=[
            pltpu.VMEM((R, batch, rows, cols, channels), BF16),
            pltpu.VMEM((2, batch, rows, 1, channels), F32),
            pltpu.VMEM((R, 2, batch, rows, 1, channels), F32),
            pltpu.VMEM(time_weight.shape, BF16),
            pltpu.VMEM((3, R * rows + 2, batch * cols, channels), BF16),
            pltpu.VMEM((R * rows, batch * cols, channels), BF16),
            pltpu.VMEM((3, 3, wide, channels), BF16),
            pltpu.VMEM((channels, 3 * inner), BF16),
            pltpu.VMEM((inner, channels), BF16),
            pltpu.VMEM((C, 8, channels), F32),
            pltpu.VMEM((R, batch * span, wide), BF16),
            pltpu.VMEM((R, batch * span, wide), BF16),
            pltpu.VMEM((batch * span, channels), F32),
            pltpu.VMEM((batch, (2 * C + 1) * span, inner), BF16),
            pltpu.VMEM((batch, (2 * C + 1) * span, inner), BF16),
            pltpu.VMEM((batch, span, inner), BF16),
            pltpu.VMEM((NX, batch, span, inner), BF16),
            pltpu.VMEM((batch, span, inner), F32),
            pltpu.VMEM((batch, span, 128), F32),
            pltpu.VMEM((NX, batch, span, inner), BF16),
            pltpu.VMEM((NX, batch, span, 128), F32),
            pltpu.VMEM((NX, batch, span, inner), BF16),
            pltpu.VMEM((NX, batch, span, 128), F32),
            pltpu.VMEM((batch, span, inner), BF16),
            dma((9,)),
            dma((batch + 2, R)),
            dma((batch + 2, R)),
            dma((1, C)),
            dma((1, C)),
            dma((C, 2, 2)),
            dma((C, 2, 2)),
            dma((2,)),
            dma((2,)),
            dma((2,)),
            dma((2,)),
            dma((5, NX)),
            dma((5, NX)),
        ],
        compiler_params=pltpu.CompilerParams(
            collective_id=0, has_side_effects=True, vmem_limit_bytes=56 * 1024 * 1024
        ),
    )(
        timestep,
        gn_gain,
        gn_bias,
        ln_gain,
        conv_bias,
        latent,
        time_weight,
        conv_weight.transpose(0, 1, 3, 2),
        q_weight,
        k_weight,
        v_weight,
        out_weight,
        stale_keys.reshape(batch, span, inner),
        stale_values.reshape(batch, span, inner),
    )
    mixed, fresh_k, fresh_v = pl.pallas_call(
        finish,
        out_shape=tuple(jax.ShapeDtypeStruct(x.shape, x.dtype) for x in (mixed, fresh_k, fresh_v)),
        in_specs=[vm] * 3,
        out_specs=(vm,) * 3,
    )(mixed, fresh_k, fresh_v)
    return (
        mixed.reshape(batch, rows, cols, channels),
        fresh_k.reshape(batch, rows, cols, inner),
        fresh_v.reshape(batch, rows, cols, inner),
    )


def solution(mesh):
    placed = (
        P("parts", "row", "col", None),
        P("parts"),
        P(),
        P(),
        P(None, None, None, "row"),
        P(),
        P(),
        P(),
        P(),
        P(),
        P(),
        P(),
        P("parts", "row", "col", None),
        P("parts", "row", "col", None),
    )
    return jax.shard_map(
        body,
        mesh=mesh,
        in_specs=placed,
        out_specs=(
            P("parts", "row", "col", None),
            P("parts", "row", "col", None),
            P("parts", "row", "col", None),
        ),
        check_vma=False,
    )
```
